128 devices in a mesh: gx: 32 (over x, y, core), gy: 4 (over z).
Axes of the slice: x: 4, y: 4, z: 4, core: 2. Of those that a mesh axis runs over, the one named last changes fastest.
Arguments:
- features: bfloat16 [32, 4, 8, 128, 128], P('gx', 'gy'), may hold values from -6 to 6
- positions: float32 [32, 4, 8, 3, 128], P('gx', 'gy'), may hold values from 0 to 1
- species: int32 [32, 4, 8, 128], P('gx', 'gy'), may hold values from 0 to 7
- atom_mask: int32 [32, 4, 8, 128], P('gx', 'gy'), may hold values 0 or 1
- charge_table: float32 [8, 64], replicated, may hold values from -5 to 5
- k_vectors: float32 [3, 512], replicated, may hold values from -1.5 to 1.5
- k_weights: float32 [512], replicated, may hold values from 0.2 to 2
- w_value: bfloat16 [2, 128, 64], replicated, may hold values from -0.5 to 0.5
- w_charge: bfloat16 [2, 128, 64], replicated, may hold values from -0.5 to 0.5
- w_radial: float32 [2, 8, 64], replicated, may hold values from -1.8 to 1.8
- w_out: bfloat16 [2, 64, 128], replicated, may hold values from -0.75 to 0.75
Outputs:
- features_out: bfloat16 [32, 4, 8, 128, 128], P('gx', 'gy')
- potential: float32 [32, 4, 8, 64, 128], P('gx', 'gy')
The draws below stay inside these ranges and needn't reach their ends.
All inputs are finite; a program needn't handle non-finite values. No bound on the sum of `atom_mask` on one device may be relied on, other than what follows from the above.
Results may differ from the reference program's by a relative error of at most 0.005.
Values may be sent and summed in bfloat16 or wider, within the bound.
No kernel may reach another device: no remote copies, remote signals or barrier semaphores. Data moves between devices by JAX's collectives and lax.ppermute only.
A program may use at most 64 MiB of HBM per device.

```python
import math
import jax
import jax.numpy as jnp
from jax import lax

D = 128
C = 64
K = 512
M = 8
NSPEC = 8
A = 128
LAYERS = 2
ZBLOCK = 4
CZ = 8
NCX = 32
NCY = 4


def set_ends(values, rng, least, high):
    longest = values.shape.index(max(values.shape))
    spots = []
    for shift in (0, 1):
        where = [jax.random.randint(jax.random.fold_in(rng, axis), (), 0, length) for axis, length in enumerate(values.shape)]
        where[longest] = (where[longest] + shift) % values.shape[longest]
        spots.append(tuple(where))
    return values.at[spots[0]].set(least).at[spots[1]].set(high)


def block_scale(own_key, dims, pieces, least, high):
    def one(position, shards_of):
        heights = jax.random.uniform(jax.random.fold_in(jax.random.fold_in(own_key, 6), position), (shards_of,), jnp.float32, least / len(pieces), high / len(pieces))
        return jnp.repeat(jnp.exp(heights), dims[position] // shards_of).reshape((-1,) + (1,) * (len(dims) - position - 1))

    level = one(*pieces[0])
    for cut in pieces[1:]:
        level = level * one(*cut)
    return level


def scatter_about(rng, shape, deviation, reach, shards=(), held_as=jnp.bfloat16):
    values = jax.random.normal(rng, shape, jnp.float32) * deviation
    if len(shards) > 0:
        values = block_scale(rng, shape, shards, -0.22, 0.18) * values
    return jnp.clip(values, min=-reach, max=reach).astype(held_as)


def setup_inputs(seed: int = 0) -> dict:
    splits = jax.random.split(jax.random.key(seed), 12)
    features = scatter_about(splits[0], (NCX, NCY, CZ, D, A), 1.0, 6.0, ((0, 32), (1, 4)))
    positions = jnp.clip(1.0 * jax.random.uniform(splits[1], (NCX, NCY, CZ, 3, A), jnp.float32) ** block_scale(splits[1], (NCX, NCY, CZ, 3, A), ((0, 32), (1, 4)), -0.2, 0.2), 0.0, 1.0)
    species = set_ends(jax.random.randint(splits[2], (NCX, NCY, CZ, A), 0, NSPEC), jax.random.fold_in(splits[2], 1), 0, NSPEC - 1).astype(jnp.int32)
    atom_mask = set_ends((jax.random.randint(splits[3], (NCX, NCY, CZ, A), 0, 4) < 3).astype(jnp.int32), jax.random.fold_in(splits[3], 1), 0, 1)
    charge_table = scatter_about(splits[4], (NSPEC, C), 1.0, 5.0, (), jnp.float32)
    k_vectors = jnp.clip(jax.random.uniform(splits[5], (3, K), jnp.float32, -1.5, 1.5), -1.5, 1.5)
    k_weights = jnp.clip(jnp.exp(jax.random.uniform(splits[6], (K,), jnp.float32, math.log(0.2), math.log(2.0))), 0.2, 2.0)
    w_value = scatter_about(splits[7], (LAYERS, D, C), D ** -0.5, 0.5)
    w_charge = scatter_about(splits[8], (LAYERS, D, C), D ** -0.5, 0.5)
    w_radial = scatter_about(splits[9], (LAYERS, M, C), 0.3, 1.8, (), jnp.float32)
    w_out = scatter_about(splits[10], (LAYERS, C, D), C ** -0.5, 0.75)
    return {"features": features, "positions": positions, "species": species, "atom_mask": atom_mask, "charge_table": charge_table, "k_vectors": k_vectors, "k_weights": k_weights, "w_value": w_value, "w_charge": w_charge, "w_radial": w_radial, "w_out": w_out}


def cell_messages(ext_pos, ext_val, radial_mix, z_index):
    atom_count = ext_pos.shape[-1]
    chan_count = ext_val.shape[-2]
    basis_count = radial_mix.shape[0]
    near_pos = lax.dynamic_slice_in_dim(ext_pos, z_index, 3, 2)
    shifts = jnp.arange(3, dtype=jnp.float32) - 1.0
    grid_shift = jnp.stack(jnp.meshgrid(shifts, shifts, shifts, indexing='ij'), axis=-1)
    near_pos = near_pos + grid_shift[..., None]
    near_pos = jnp.moveaxis(near_pos, 3, 0).reshape(3, 27 * atom_count)
    centre = lax.dynamic_index_in_dim(ext_pos[1, 1], z_index + 1, 0, keepdims=False)
    offset_vec = near_pos[:, None, :] - centre[:, :, None]
    dist_sq = lax.optimization_barrier(jnp.sum(offset_vec * offset_vec, axis=0))
    row_ids = lax.broadcasted_iota(jnp.int32, dist_sq.shape, 0)
    col_ids = lax.broadcasted_iota(jnp.int32, dist_sq.shape, 1)
    keep = (dist_sq < 1.0) & (col_ids != row_ids + 13 * atom_count)
    envelope = jnp.where(keep, jnp.square(1.0 - dist_sq), 0.0)
    radius = jnp.sqrt(dist_sq)
    centres = (jnp.arange(basis_count, dtype=jnp.float32) + 0.5) / basis_count
    basis_vals = (jnp.exp(-jnp.square((radius[None] - centres[:, None, None]) * basis_count)) * envelope[None]).astype(jnp.bfloat16)
    near_val = lax.dynamic_slice_in_dim(ext_val, z_index, 3, 2)
    near_val = jnp.moveaxis(near_val.reshape(27, chan_count, atom_count), 1, 0).reshape(chan_count, 27 * atom_count)
    partial_value = jnp.einsum('mab,cb->mca', basis_vals.astype(jnp.float32), near_val.astype(jnp.float32))
    return jnp.einsum('mc,mca->ca', radial_mix, partial_value, precision=lax.Precision.HIGHEST)

def column_messages(ext_pos, ext_val, radial_mix, block_size):
    cell_count = ext_pos.shape[2] - 2

    def one_block(block_start):
        z_ids = block_start + jnp.arange(block_size, dtype=jnp.int32)
        return jax.vmap(lambda z_index: cell_messages(ext_pos, ext_val, radial_mix, z_index))(z_ids)
    starts = jnp.arange(0, cell_count, block_size, dtype=jnp.int32)
    result = lax.map(one_block, starts)
    return result.reshape(cell_count, ext_val.shape[3], ext_val.shape[4])

def wrap_pad(array):
    array = jnp.concatenate([array[-1:], array, array[:1]], axis=0)
    array = jnp.concatenate([array[:, -1:], array, array[:, :1]], axis=1)
    return jnp.pad(array, ((0, 0), (0, 0), (1, 1), (0, 0), (0, 0)))

def reference(features, positions, species, atom_mask, charge_table, k_vectors, k_weights, w_value, w_charge, w_radial, w_out):
    highest = lax.Precision.HIGHEST
    size_x, size_y, cell_count = (features.shape[0], features.shape[1], features.shape[2])
    atom_count = features.shape[4]
    chan_count = w_value.shape[2]
    kcount = k_vectors.shape[1]
    live = atom_mask.astype(jnp.float32)
    live_wide = live[:, :, :, None, :]
    onehot = (species[:, :, :, None, :] == jnp.arange(NSPEC, dtype=jnp.int32)[:, None]).astype(jnp.float32)
    offsets = jnp.einsum('sc,xyzsa->xyzca', charge_table, onehot, precision=highest)
    grid_x = jnp.broadcast_to(jnp.arange(size_x, dtype=jnp.float32)[:, None, None], (size_x, size_y, cell_count))
    grid_y = jnp.broadcast_to(jnp.arange(size_y, dtype=jnp.float32)[None, :, None], (size_x, size_y, cell_count))
    grid_z = jnp.broadcast_to(jnp.arange(cell_count, dtype=jnp.float32)[None, None, :], (size_x, size_y, cell_count))
    anchor = jnp.stack([grid_x, grid_y, grid_z], axis=-1)
    absolute = positions + anchor[..., None]
    abs_cols = absolute.reshape(size_x * size_y, cell_count, 3, atom_count)
    ewald_scale = 1.0 / math.sqrt(kcount * size_x * size_y * cell_count * atom_count)
    pos_pad = wrap_pad(positions)
    zero = jnp.zeros((), jnp.int32)

    def trig_of(column):
        phases = jnp.einsum('dk,zda->kza', k_vectors, column, precision=highest).reshape(kcount, cell_count * atom_count)
        return (jnp.cos(phases), jnp.sin(phases))
    hidden = features
    potential = jnp.zeros((size_x, size_y, cell_count, chan_count, atom_count), jnp.float32)
    for layer in range(LAYERS):
        values_all = jnp.einsum('dc,xyzda->xyzca', w_value[layer].astype(jnp.float32), hidden.astype(jnp.float32)).astype(jnp.bfloat16) * live_wide.astype(jnp.bfloat16)
        charges = (jnp.einsum('dc,xyzda->xyzca', w_charge[layer].astype(jnp.float32), hidden.astype(jnp.float32)) + offsets) * live_wide
        charge_cols = jnp.moveaxis(charges.reshape(size_x * size_y, cell_count, chan_count, atom_count), 2, 1).reshape(size_x * size_y, chan_count, cell_count * atom_count)

        def add_column(carry, inputs):
            column, charge_col = inputs
            cos_t, sin_t = trig_of(column)
            return ((carry[0] + jnp.dot(charge_col, cos_t.T, precision=highest, preferred_element_type=jnp.float32), carry[1] + jnp.dot(charge_col, sin_t.T, precision=highest, preferred_element_type=jnp.float32)), None)
        start_sums = (jnp.zeros((chan_count, kcount), jnp.float32), jnp.zeros((chan_count, kcount), jnp.float32))
        (s_cos, s_sin), _ = lax.scan(add_column, start_sums, (abs_cols, charge_cols))
        weighted_cos = s_cos * k_weights[None, :]
        weighted_sin = s_sin * k_weights[None, :]

        def column_potential(column):
            cos_t, sin_t = trig_of(column)
            total = jnp.dot(weighted_cos, cos_t, precision=highest, preferred_element_type=jnp.float32) + jnp.dot(weighted_sin, sin_t, precision=highest, preferred_element_type=jnp.float32)
            return jnp.moveaxis((total * ewald_scale).reshape(chan_count, cell_count, atom_count), 0, 1)
        potential = lax.map(column_potential, abs_cols).reshape(size_x, size_y, cell_count, chan_count, atom_count)
        val_pad = wrap_pad(values_all)

        def one_column(flat):
            index_x = (flat // size_y).astype(jnp.int32)
            index_y = (flat % size_y).astype(jnp.int32)
            ext_pos = lax.dynamic_slice(pos_pad, (index_x, index_y, zero, zero, zero), (3, 3, cell_count + 2, 3, atom_count))
            ext_val = lax.dynamic_slice(val_pad, (index_x, index_y, zero, zero, zero), (3, 3, cell_count + 2, chan_count, atom_count))
            return column_messages(ext_pos, ext_val, w_radial[layer], ZBLOCK)
        radial = lax.map(one_column, jnp.arange(size_x * size_y, dtype=jnp.int32)).reshape(size_x, size_y, cell_count, chan_count, atom_count)
        activated = jax.nn.silu(radial + potential).astype(jnp.bfloat16)
        update = jnp.einsum('cd,xyzca->xyzda', w_out[layer].astype(jnp.float32), activated.astype(jnp.float32))
        hidden = (hidden.astype(jnp.float32) + update * live_wide).astype(jnp.bfloat16)
    return (hidden, potential)
```

```python
import math

import jax
import jax.numpy as jnp
from jax import lax
from jax.experimental import pallas as pl
from jax.experimental.pallas import tpu as pltpu
from jax.sharding import PartitionSpec as P

F32 = jnp.float32
BF = jnp.bfloat16
CZ = 8
A = 128
D = 128
C = 64
K = 512
M = 8
NSPEC = 8
NX, NY, NC, NZ = 4, 4, 2, 4
LOG2E = math.log2(math.e)
SCALE = math.sqrt(64.0 * LOG2E)
EDGE = 64.0 * LOG2E
SIN_C = (3.14159264, -5.16771009, 2.55007766, -0.59829216, 0.07765941)
COS_C = (0.99999995, -4.93479286, 4.05841191, -1.33188016, 0.21969679)
MSG = CZ * C + 80
BIG = pltpu.CompilerParams(vmem_limit_bytes=60 << 20)
AXES = ("gx", "gy")
ORDERS = ("zyx", "yxz")
STEPS = [(z, d) for z in range(CZ) for d in (-1, 0, 1) if 0 <= z + d < CZ]
NT = (((1,), (1,)), ((), ()))
NN = (((1,), (0,)), ((), ()))


def dot(a, b, dims=NN):
    return lax.dot_general(a, b, dims, preferred_element_type=F32)


def split2(x):
    hi = x.astype(BF)
    return hi, (x - hi.astype(F32)).astype(BF)


def prep_kernel(feat, pos, spec, mask, table, wv, wq, msg, q_ref, off_ref):
    wt = jnp.concatenate([wv[...].astype(F32), wq[...].astype(F32)], axis=1).T.astype(BF)
    tt = table[...].T
    for z in range(CZ):
        live = mask[z : z + 1, :].astype(F32)
        both = dot(wt, feat[z])
        msg[z * C : (z + 1) * C, :] = (both[:C] * live).astype(BF)
        sp = spec[z : z + 1, :]
        off = jnp.zeros((C, A), F32)
        for s in range(NSPEC):
            off = jnp.where(sp == s, tt[:, s : s + 1], off)
        off_ref[:, z * A : (z + 1) * A] = off
        q_ref[:, z * A : (z + 1) * A] = (both[C:] + off) * live
    pieces = [[], [], []]
    for d in range(3):
        p = pos[:, d, :]
        hi = p.astype(BF).astype(F32)
        mid = (p - hi).astype(BF).astype(F32)
        pieces[0].append(hi)
        pieces[1].append(mid)
        pieces[2].append(p - hi - mid)
    rows = pieces[0] + pieces[1] + pieces[2] + [jnp.zeros((8, A), F32)]
    msg[CZ * C :, :] = jnp.concatenate(rows, axis=0).astype(BF)


def sums(q, th, tl):
    qh, ql = split2(q)
    both = dot(jnp.concatenate([qh, ql], axis=0), th, NT)
    return both[:C] + both[C:] + dot(qh, tl, NT)


def put_halves(s_ref, s, ci, keep, send):
    s_ref[...] = s
    h = C // 2
    keep[...] = s_ref[pl.ds(pl.multiple_of(ci * h, h), h), :]
    send[...] = s_ref[pl.ds(pl.multiple_of((1 - ci) * h, h), h), :].astype(BF)


def trig_kernel(meta, pos, kvec, q, th, tl, keep, send, s_ref):
    k8 = jnp.concatenate([kvec[...] * (1.0 / (2.0 * math.pi)), jnp.zeros((5, K), F32)], axis=0)
    kt = k8.T
    gx = meta[0].astype(F32)
    gy = meta[1].astype(F32)
    rows = 128
    for i in range(K // rows):
        kx = jnp.broadcast_to(kt[i * rows : (i + 1) * rows, 0:1], (rows, A))
        ky = jnp.broadcast_to(kt[i * rows : (i + 1) * rows, 1:2], (rows, A))
        kz = jnp.broadcast_to(kt[i * rows : (i + 1) * rows, 2:3], (rows, A))
        for z in range(CZ):
            px = pos[z, 0:1, :] + gx
            py = pos[z, 1:2, :] + gy
            pz = pos[z, 2:3, :] + float(z)
            t = kx * px + ky * py + kz * pz
            u = t - jnp.round(t)
            v = u * u
            s = jnp.full((), SIN_C[4], F32)
            c = jnp.full((), COS_C[4], F32)
            for n in (3, 2, 1, 0):
                s = s * v + SIN_C[n]
                c = c * v + COS_C[n]
            s = s * u
            s2 = s + s
            sin = s2 * c
            cos = 1.0 - s2 * s
            r0 = i * rows
            cols = slice(z * A, (z + 1) * A)
            h, low = split2(cos)
            th[r0 : r0 + rows, cols] = h
            tl[r0 : r0 + rows, cols] = low
            h, low = split2(sin)
            th[K + r0 : K + r0 + rows, cols] = h
            tl[K + r0 : K + r0 + rows, cols] = low
    put_halves(s_ref, sums(q[...], th[...], tl[...]), meta[2], keep, send)


def pair_kernel(shifts, first_self, meta, *refs):
    n = len(shifts)
    own_pos, wr = refs[0], refs[1]
    vals = refs[2 : 2 + n]
    poss = refs[2 + n : 2 + 2 * n]
    out = refs[2 + 2 * n]
    planes, ft, gs, buf0, buf1, acc = refs[3 + 2 * n :]
    sign = (1 - 2 * meta[2]).astype(F32)

    def coords(ref):
        x = ref[CZ * C :, :].astype(F32)
        return [(x[8 * d : 8 * d + 8] + x[24 + 8 * d : 32 + 8 * d]) + x[48 + 8 * d : 56 + 8 * d] for d in range(3)]

    def pieces(x):
        hi = x.astype(BF).astype(F32)
        rest = x - hi
        mid = rest.astype(BF).astype(F32)
        return hi, mid, rest - mid

    one = jnp.ones((CZ, A), F32)
    local = coords(own_pos)
    for di, dz in enumerate((-1, 0, 1)):
        x = [(local[0] - 0.5) * SCALE, (local[1] - 0.5) * SCALE, (local[2] - (0.5 + dz)) * SCALE]
        parts = [pieces(v) for v in x]
        norm = pieces(x[0] * x[0] + x[1] * x[1] + x[2] * x[2])
        rows = []
        for j in (0, 0, 1, 0, 2, 1):
            rows += [-2.0 * parts[d][j] for d in range(3)]
        rows += [one, one, one] + list(norm)
        for r, v in enumerate(rows):
            planes[r] = v
        for z in range(CZ):
            gs[di * CZ + z] = planes[:, z, :].astype(BF)
    for col in range(n):
        times, oy = shifts[col]
        p = coords(poss[col])
        x = [(p[0] + (sign * times - 0.5)) * SCALE, (p[1] + (oy - 0.5)) * SCALE, (p[2] - 0.5) * SCALE]
        parts = [pieces(v) for v in x]
        norm = pieces(x[0] * x[0] + x[1] * x[1] + x[2] * x[2])
        rows = []
        for j in (0, 1, 0, 2, 0, 1):
            rows += [parts[d][j] for d in range(3)]
        rows += list(norm) + [one, one, one]
        for r, v in enumerate(rows):
            planes[r] = v
        for z in range(CZ):
            ft[col * CZ + z] = planes[:, z, :].T.astype(BF)
    acc[...] = jnp.zeros_like(acc)
    row_ids = lax.broadcasted_iota(jnp.int32, (A, A), 0)
    col_ids = lax.broadcasted_iota(jnp.int32, (A, A), 1)

    def basis(t, buf, col):
        z, dz = meta[4 + t], meta[4 + len(STEPS) + t]
        g = gs[(dz + 1) * CZ + z]
        r2 = dot(ft[col * CZ + z + dz], g)
        if first_self and col == 0:
            r2 = jnp.where(row_ids == col_ids + dz * 1024, EDGE, r2)
        r2 = jnp.minimum(jnp.maximum(r2, 1e-12), EDGE)
        h = r2 * lax.rsqrt(r2) * math.sqrt(LOG2E)
        ratio = jnp.exp2(h + h)
        e = EDGE - r2
        w = jnp.exp2(h - r2) * (e * e)
        for m in range(M):
            buf[m // 2, col * A : (col + 1) * A, (m % 2) * A : (m % 2 + 1) * A] = w.astype(BF)
            if m < M - 1:
                w = w * ratio

    def product(t, buf, j):
        z, dz = meta[4 + t], meta[4 + len(STEPS) + t]
        rows = pl.ds(pl.multiple_of((z + dz) * C, C), C)
        v = jnp.concatenate([ref[rows, :] for ref in vals], axis=1)
        acc[z, :, 2 * j * A : 2 * (j + 1) * A] += dot(v, buf[j])

    def half(t_new, buf_new, t_old, buf_old, new, old):
        if n >= 4:
            at = {((j + 1) * n) // 5: j for j in range(4)}
            for col in range(n):
                if new:
                    basis(t_new, buf_new, col)
                if old and col in at:
                    product(t_old, buf_old, at[col])
        else:
            for col in range(n):
                if new:
                    basis(t_new, buf_new, col)
                if old:
                    for j in range(4):
                        if j * n // 4 == col:
                            product(t_old, buf_old, j)

    total = len(STEPS)
    half(0, buf0, 0, buf1, True, False)

    def body(i, carry):
        t = 2 * i
        half(t + 1, buf1, t, buf0, True, True)
        half(t + 2, buf0, t + 1, buf1, True, True)
        return carry

    lax.fori_loop(0, total // 2 - 1, body, 0)
    half(total - 1, buf1, total - 2, buf0, True, True)
    half(0, buf0, total - 1, buf1, False, True)
    mix = jnp.concatenate(
        [wr[m : m + 1, :] * (math.exp(-((m + 0.5) ** 2)) / EDGE**2) for m in range(M)], axis=0
    ).T
    for z in range(CZ):
        r = jnp.zeros((C, A), F32)
        for m in range(M):
            r = r + acc[z, :, m * A : (m + 1) * A] * mix[:, m : m + 1]
        out[z] = r


def post_common(meta, keep, got, kw, th, tl, s_ref):
    ci = meta[2]
    h = C // 2
    s_ref[pl.ds(pl.multiple_of(ci * h, h), h), :] = keep[...]
    s_ref[pl.ds(pl.multiple_of((1 - ci) * h, h), h), :] = got[...].astype(F32)
    scale = 1.0 / math.sqrt(K * NX * NY * NC * NZ * CZ * A)
    k2 = jnp.concatenate([kw[...], kw[...]], axis=1) * scale
    wh, wl = split2(s_ref[...] * k2)
    both = dot(jnp.concatenate([wh, wl], axis=0), th[...])
    return both[:C] + both[C:] + dot(wh, tl[...])


def update(hid, pot, rads, mask, wot, z):
    r = rads[0][z]
    for ref in rads[1:]:
        r = r + ref[z]
    x = r + pot[:, z * A : (z + 1) * A]
    act = (x / (1.0 + jnp.exp(-x))).astype(BF)
    live = mask[z : z + 1, :].astype(F32)
    return (hid[z].astype(F32) + dot(wot, act) * live).astype(BF)


def middle_kernel(nr, meta, keep, got, kw, th, tl, hid, mask, off, wo, wv, wq, *refs):
    rads = refs[:nr]
    new_hid, vals, keep1, send1, s_ref, q_ref = refs[nr:]
    pot = post_common(meta, keep, got, kw, th, tl, s_ref)
    wot = wo[...].astype(F32).T.astype(BF)
    wt = jnp.concatenate([wv[...].astype(F32), wq[...].astype(F32)], axis=1).T.astype(BF)
    for z in range(CZ):
        h = update(hid, pot, rads, mask, wot, z)
        new_hid[z] = h
        live = mask[z : z + 1, :].astype(F32)
        both = dot(wt, h)
        vals[z * C : (z + 1) * C, :] = (both[:C] * live).astype(BF)
        q_ref[:, z * A : (z + 1) * A] = (both[C:] + off[:, z * A : (z + 1) * A]) * live
    put_halves(s_ref, sums(q_ref[...], th[...], tl[...]), meta[2], keep1, send1)


def last_kernel(nr, meta, keep, got, kw, th, tl, hid, mask, wo, *refs):
    rads = refs[:nr]
    new_hid, pot_out, s_ref = refs[nr:]
    pot = post_common(meta, keep, got, kw, th, tl, s_ref)
    wot = wo[...].astype(F32).T.astype(BF)
    for z in range(CZ):
        pot_out[z] = pot[:, z * A : (z + 1) * A]
        new_hid[z] = update(hid, pot, rads, mask, wot, z)


SMEM = pl.BlockSpec(memory_space=pltpu.SMEM)
VM = pl.BlockSpec(memory_space=pltpu.VMEM)


def call(kernel, outs, scratch, args, flops, name, smem=True):
    specs = [SMEM if (smem and i == 0) else VM for i in range(len(args))]
    return pl.pallas_call(
        kernel,
        out_shape=[jax.ShapeDtypeStruct(s, d) for s, d in outs],
        in_specs=specs,
        out_specs=[VM] * len(outs),
        scratch_shapes=scratch,
        compiler_params=BIG,
        cost_estimate=pl.CostEstimate(flops=flops, bytes_accessed=1 << 20, transcendentals=0),
        name=name,
    )(*args)


def pairs(meta, own_pos, wr, cols, name, first_self):
    n = len(cols)
    shifts = [c[2] for c in cols]
    args = [meta, own_pos, wr] + [c[0] for c in cols] + [c[1] for c in cols]
    scratch = [
        pltpu.VMEM((24, CZ, A), F32),
        pltpu.VMEM((n * CZ, A, 24), BF),
        pltpu.VMEM((3 * CZ, 24, A), BF),
        pltpu.VMEM((4, n * A, 2 * A), BF),
        pltpu.VMEM((4, n * A, 2 * A), BF),
        pltpu.VMEM((CZ, C, M * A), F32),
    ]
    return call(
        lambda *r: pair_kernel(shifts, first_self, *r),
        [((CZ, C, A), F32)],
        scratch,
        args,
        n * 700_000_000,
        name,
    )[0]


def flat(fn):
    pairs_ = []
    for x in range(NX):
        for y in range(NY):
            for c in range(NC):
                for z in range(NZ):
                    a, b, e, f = fn(x, y, c, z)
                    pairs_.append((((x * NY + y) * NC + c) * NZ + z, ((a * NY + b) * NC + e) * NZ + f))
    return pairs_


def moved(x, y, c, z, axis, k):
    at = {"x": x, "y": y, "z": z}
    at[axis] ^= k
    return at["x"], at["y"], c, at["z"]


PARTNER = [(i, i ^ 1) for i in range(NX * NY * NC)]
OTHER = [(i, (i + (1 if i % 2 else -1)) % (NX * NY * NC)) for i in range(NX * NY * NC)]


def all_sum(keep, send):
    got = lax.ppermute(send, "gx", PARTNER)
    y = keep + got.astype(F32)
    for stage in range(3):
        b = y.astype(BF)
        y = b.astype(F32)
        for k in (1, 2, 3):
            perm = flat(lambda x, yy, c, z: moved(x, yy, c, z, ORDERS[c][stage], k))
            y = y + lax.ppermute(b, AXES, perm).astype(F32)
    return y, lax.ppermute(y.astype(BF), "gx", PARTNER)


def halo(own):
    up = [(i, (i + 1) % NZ) for i in range(NZ)]
    down = [(j, i) for i, j in up]
    before = lax.ppermute(own, "gy", up)
    after = lax.ppermute(own, "gy", down)
    three = jnp.concatenate([own[None], before[None], after[None]], axis=0)
    part = lax.ppermute(three, "gx", PARTNER)
    other = lax.ppermute(three, "gx", OTHER)
    return before, after, part, other


def on_device(feat, pos, spec, mask, table, kvec, kw, wv, wq, wr, wo):
    feat, pos, spec, mask = feat[0, 0], pos[0, 0], spec[0, 0], mask[0, 0]
    gx, gy = lax.axis_index("gx"), lax.axis_index("gy")
    steps = jnp.array([z for z, _ in STEPS] + [d for _, d in STEPS], jnp.int32)
    meta = jnp.concatenate([jnp.stack([gx, gy, gx % 2, gx * 0]).astype(jnp.int32), steps])
    kw = kw[None, :]
    half = [((C // 2, 2 * K), F32), ((C // 2, 2 * K), BF)]
    msg, q, off = call(
        prep_kernel,
        [((MSG, A), BF), ((C, CZ * A), F32), ((C, CZ * A), F32)],
        [],
        [feat, pos, spec, mask, table, wv[0], wq[0]],
        300_000_000,
        "prep",
        smem=False,
    )
    before, after, part, other = halo(msg)
    th, tl, keep, send = call(
        trig_kernel,
        [((2 * K, CZ * A), BF), ((2 * K, CZ * A), BF)] + half,
        [pltpu.VMEM((C, 2 * K), F32)],
        [meta, pos, kvec, q],
        3_000_000_000,
        "trig",
    )
    near = [(msg, (0, 0)), (before, (0, -1)), (after, (0, 1))]
    far = [(part[i], (1, (0, -1, 1)[i])) for i in range(3)] + [(other[i], (-1, (0, -1, 1)[i])) for i in range(3)]

    def radial(layer, near_v, far_v):
        a = pairs(meta, msg, wr[layer], [(v, p, s) for v, (p, s) in zip(near_v, near)], "near", True)
        b = pairs(meta, msg, wr[layer], [(v, p, s) for v, (p, s) in zip(far_v, far)], "far", False)
        return [a, b]

    rads = radial(0, [p for p, _ in near], [p for p, _ in far])
    keep, got = all_sum(keep, send)
    hid, vals, keep, send = call(
        lambda *r: middle_kernel(2, *r),
        [((CZ, D, A), BF), ((CZ * C, A), BF)] + half,
        [pltpu.VMEM((C, 2 * K), F32), pltpu.VMEM((C, CZ * A), F32)],
        [meta, keep, got, kw, th, tl, feat, mask, off, wo[0], wv[1], wq[1]] + rads,
        3_000_000_000,
        "middle",
    )
    before, after, part, other = halo(vals)
    rads = radial(1, [vals, before, after], [part[i] for i in range(3)] + [other[i] for i in range(3)])
    keep, got = all_sum(keep, send)
    hid, pot = call(
        lambda *r: last_kernel(2, *r),
        [((CZ, D, A), BF), ((CZ, C, A), F32)],
        [pltpu.VMEM((C, 2 * K), F32)],
        [meta, keep, got, kw, th, tl, hid, mask, wo[1]] + rads,
        2_000_000_000,
        "last",
    )
    return hid[None, None], pot[None, None]


def solution(mesh):
    column = P("gx", "gy")
    in_specs = (column,) * 4 + (P(),) * 7
    return jax.shard_map(on_device, mesh=mesh, in_specs=in_specs, out_specs=(column, column), check_vma=False)
```

```python
import math

import jax
import jax.numpy as jnp
from jax import lax
from jax.experimental import pallas as pl
from jax.experimental.pallas import tpu as pltpu
from jax.sharding import PartitionSpec as P

F32 = jnp.float32
BF = jnp.bfloat16
CZ = 8
A = 128
D = 128
C = 64
K = 512
M = 8
NSPEC = 8
NX, NY, NC, NZ = 4, 4, 2, 4
LOG2E = math.log2(math.e)
SCALE = math.sqrt(64.0 * LOG2E)
EDGE = 64.0 * LOG2E
SIN_C = (3.14159264, -5.16771009, 2.55007766, -0.59829216, 0.07765941)
COS_C = (0.99999995, -4.93479286, 4.05841191, -1.33188016, 0.21969679)
MSG = CZ * C + 80
AXES = ("gx", "gy")
ORDERS = ("zyx", "yxz")
NT = (((1,), (1,)), ((), ()))
NN = (((1,), (0,)), ((), ()))


def dot(a, b, dims=NN):
    return lax.dot_general(a, b, dims, preferred_element_type=F32)


def split2(x):
    hi = x.astype(BF)
    return hi, (x - hi.astype(F32)).astype(BF)


def pieces(x):
    hi = x.astype(BF).astype(F32)
    rest = x - hi
    mid = rest.astype(BF).astype(F32)
    return hi, mid, rest - mid


def core():
    return lax.rem(lax.axis_index("gx"), 2)


def sums(q, th, tl):
    qh, ql = split2(q)
    both = dot(jnp.concatenate([qh, ql], axis=0), th, NT)
    return both[:C] + both[C:] + dot(qh, tl, NT)


def put_halves(s_ref, s, keep, send):
    s_ref[...] = s
    h = C // 2
    ci = core()
    keep[...] = s_ref[pl.ds(pl.multiple_of(ci * h, h), h), :]
    send[...] = s_ref[pl.ds(pl.multiple_of((1 - ci) * h, h), h), :].astype(BF)


def first_kernel(*refs):
    feat, pos, spec, mask, table, kvec, wv, wq = refs[:8]
    msg, off_ref, th, tl, keep, send, s_ref, q_ref = refs[8:]
    wt = jnp.concatenate([wv[0], wq[0]], axis=0)
    tt = table[...].T
    for z in range(CZ):
        live = mask[z : z + 1, :].astype(F32)
        both = dot(wt, feat[z])
        msg[z * C : (z + 1) * C, :] = (both[:C] * live).astype(BF)
        sp = spec[z : z + 1, :]
        off = jnp.zeros((C, A), F32)
        for s in range(NSPEC):
            off = jnp.where(sp == s, tt[:, s : s + 1], off)
        off_ref[:, z * A : (z + 1) * A] = off
        q_ref[:, z * A : (z + 1) * A] = (both[C:] + off) * live
    parts = [pieces(pos[d]) for d in range(3)]
    rows = [parts[d][j] for j in range(3) for d in range(3)] + [jnp.zeros((8, A), F32)]
    msg[CZ * C :, :] = jnp.concatenate(rows, axis=0).astype(BF)
    k8 = jnp.concatenate([kvec[...] * (1.0 / (2.0 * math.pi)), jnp.zeros((5, K), F32)], axis=0)
    kt = k8.T
    gx = lax.axis_index("gx").astype(F32)
    gy = lax.axis_index("gy").astype(F32)
    rows = 64
    for i in range(K // rows):
        kx = jnp.broadcast_to(kt[i * rows : (i + 1) * rows, 0:1], (rows, A))
        ky = jnp.broadcast_to(kt[i * rows : (i + 1) * rows, 1:2], (rows, A))
        kz = jnp.broadcast_to(kt[i * rows : (i + 1) * rows, 2:3], (rows, A))
        for z in range(CZ):
            px = pos[0, z : z + 1, :] + gx
            py = pos[1, z : z + 1, :] + gy
            pz = pos[2, z : z + 1, :] + float(z)
            t = kx * px + ky * py + kz * pz
            u = t - jnp.round(t)
            v = u * u
            s = jnp.full((), SIN_C[4], F32)
            c = jnp.full((), COS_C[4], F32)
            for n in (3, 2, 1, 0):
                s = s * v + SIN_C[n]
                c = c * v + COS_C[n]
            s = s * u
            s2 = s + s
            sin = s2 * c
            cos = 1.0 - s2 * s
            r0 = i * rows
            cols = slice(z * A, (z + 1) * A)
            h, low = split2(cos)
            th[r0 : r0 + rows, cols] = h
            tl[r0 : r0 + rows, cols] = low
            h, low = split2(sin)
            th[K + r0 : K + r0 + rows, cols] = h
            tl[K + r0 : K + r0 + rows, cols] = low
    put_halves(s_ref, sums(q_ref[...], th[...], tl[...]), keep, send)


WHERE = 1
PARTS = 1
CHUNK = CZ // PARTS
N_COL = 9
SHIFTS = [(0, 0), (0, -1), (0, 1)] + [(1, d) for d in (0, -1, 1)] + [(-1, d) for d in (0, -1, 1)]
ROWS = 24 * CZ
PRODUCTS = {0: 0, 2: 1, 4: 2, 6: 3}


def nine(own, before, after, part, other):
    return [own, before, after] + [part.at[i] for i in range(3)] + [other.at[i] for i in range(3)]


def sides(x, times, order, tail):
    parts = [pieces(v) for v in x]
    norm = list(pieces(x[0] * x[0] + x[1] * x[1] + x[2] * x[2]))
    one = [jnp.ones((CZ, A), F32)] * 3
    rows = [parts[d][j] if times == 1.0 else times * parts[d][j] for j in order for d in range(3)]
    return jnp.concatenate(rows + (one + norm if tail else norm + one), axis=0)


def geometry_kernel(own, before, after, part, other, ft, gs):
    sign = (1 - 2 * core()).astype(F32)

    def coords(ref):
        x = ref[CZ * C :, :].astype(F32)
        return [(x[8 * d : 8 * d + 8] + x[24 + 8 * d : 32 + 8 * d]) + x[48 + 8 * d : 56 + 8 * d] for d in range(3)]

    level = lax.rem(lax.broadcasted_iota(jnp.int32, (ROWS, A), 0), CZ)
    local = coords(own)
    for di, dz in enumerate((-1, 0, 1)):
        x = local if dz == 0 else [pltpu.roll(v, dz % CZ, 0) for v in local]
        x = [(x[0] - 0.5) * SCALE, (x[1] - 0.5) * SCALE, (x[2] - (0.5 + dz)) * SCALE]
        side = sides(x, -2.0, (0, 0, 1, 0, 2, 1), True)
        for zb in range(CZ):
            gs[di * CZ + zb] = jnp.where(level == zb, side, 0.0).astype(BF)
    for col, ref in enumerate(nine(own, before, after, part, other)):
        times, oy = SHIFTS[col]
        p = coords(ref)
        x = [(p[0] + (sign * times - 0.5)) * SCALE, (p[1] + (oy - 0.5)) * SCALE, (p[2] - 0.5) * SCALE]
        ft[col * A : (col + 1) * A, :] = sides(x, 1.0, (0, 1, 0, 2, 0, 1), False).T.astype(BF)


def pair_kernel(layer, z0, nz, ft, gs, wr, *refs):
    out, acc = refs[-2], refs[-1]
    vals = nine(*refs[:-2])
    u0 = max(3 * z0, 1)
    total = min(3 * (z0 + nz), 3 * CZ - 1) - u0
    row_ids = lax.broadcasted_iota(jnp.int32, (A, A), 0)
    col_ids = lax.broadcasted_iota(jnp.int32, (A, A), 1)

    def step(t):
        u = jnp.minimum(t, total - 1) + u0
        return lax.div(u, 3), lax.rem(u, 3) - 1

    def body_with(r0, r1, b0, b1):
        rbuf, bbuf = (r0, r1), (b0, b1)

        def distance(p, gen):
            (z, dz), (z1, dz1) = step(2 * p), step(2 * p + 1)
            both = jnp.concatenate([gs[(dz + 1) * CZ + z + dz], gs[(dz1 + 1) * CZ + z1 + dz1]], axis=1)
            r2 = dot(ft[...], both)
            for i, d in enumerate((dz, dz1)):
                part = r2[:, i * A : (i + 1) * A]
                rbuf[gen][i, :A] = jnp.where(row_ids == col_ids + d * 1024, EDGE, part[:A])
                rbuf[gen][i, A:] = part[A:]

        def basis(gen, par, col):
            for r0 in range(col * A, (col + 1) * A, 16):
                r2 = jnp.minimum(jnp.maximum(rbuf[gen][par, r0 : r0 + 16], 1e-12), EDGE)
                h = r2 * lax.rsqrt(r2) * math.sqrt(LOG2E)
                ratio = jnp.exp2(h + h)
                e = EDGE - r2
                w = jnp.exp2(h - r2) * (e * e)
                for m in range(M):
                    bbuf[par][m // 2, r0 : r0 + 16, (m % 2) * A : (m % 2 + 1) * A] = w.astype(BF)
                    if m < M - 1:
                        w = w * ratio

        def product(t, par, j):
            z, dz = step(t)
            rows = pl.ds(pl.multiple_of((z + dz) * C, C), C)
            v = jnp.concatenate([ref[rows, :] for ref in vals], axis=1)
            acc[z - z0, :, 2 * j * A : 2 * (j + 1) * A] += dot(v, bbuf[par][j])

        def two(p, gen, old=True):
            for par in (0, 1):
                for col in range(N_COL):
                    basis(gen, par, col)
                    if par == 0 and col == WHERE:
                        distance(p + 1, 1 - gen)
                    if (old or par == 1) and col in PRODUCTS:
                        product(2 * p + par - 1, 1 - par, PRODUCTS[col])

        distance(0, 0)
        acc[...] = jnp.zeros_like(acc)
        two(0, 0, old=False)

        def body(i, carry):
            two(2 * i + 1, 1)
            two(2 * i + 2, 0)
            return carry

        lax.fori_loop(0, (total // 2 - 1) // 2, body, 0)
        for j in range(4):
            product(total - 1, 1, j)

    pl.run_scoped(
        body_with,
        pltpu.VMEM((2, N_COL * A, A), F32),
        pltpu.VMEM((2, N_COL * A, A), F32),
        pltpu.VMEM((4, N_COL * A, 2 * A), BF),
        pltpu.VMEM((4, N_COL * A, 2 * A), BF),
    )
    mix = jnp.concatenate(
        [wr[layer, m : m + 1, :] * (math.exp(-((m + 0.5) ** 2)) / EDGE**2) for m in range(M)], axis=0
    ).T
    for z in range(nz):
        r = jnp.zeros((C, A), F32)
        for m in range(M):
            r = r + acc[z, :, m * A : (m + 1) * A] * mix[:, m : m + 1]
        out[z] = r


def the_potential(keep, got, kw, th, tl, s_ref):
    ci = core()
    h = C // 2
    s_ref[pl.ds(pl.multiple_of(ci * h, h), h), :] = keep[...]
    s_ref[pl.ds(pl.multiple_of((1 - ci) * h, h), h), :] = got[...].astype(F32)
    scale = 1.0 / math.sqrt(K * NX * NY * NC * NZ * CZ * A)
    k2 = jnp.concatenate([kw[...], kw[...]], axis=1) * scale
    wh, wl = split2(s_ref[...] * k2)
    both = dot(jnp.concatenate([wh, wl], axis=0), th[...])
    return both[:C] + both[C:] + dot(wh, tl[...])


def updated(hid, pot, rad, mask, wot, z):
    x = rad[z // CHUNK][z % CHUNK] + pot[:, z * A : (z + 1) * A]
    act = (x / (1.0 + jnp.exp(-x))).astype(BF)
    live = mask[z : z + 1, :].astype(F32)
    return (hid[z].astype(F32) + dot(wot, act) * live).astype(BF)


def middle_kernel(keep, got, kw, th, tl, hid, mask, off, wo, wv, wq, *refs):
    rad = refs[:PARTS]
    new_hid, vals, keep1, send1, s_ref, q_ref = refs[PARTS:]
    pot = the_potential(keep, got, kw, th, tl, s_ref)
    wot = wo[0].astype(F32).T.astype(BF)
    wt = jnp.concatenate([wv[1], wq[1]], axis=0)
    for z in range(CZ):
        h = updated(hid, pot, rad, mask, wot, z)
        new_hid[z] = h
        live = mask[z : z + 1, :].astype(F32)
        both = dot(wt, h)
        vals[z * C : (z + 1) * C, :] = (both[:C] * live).astype(BF)
        q_ref[:, z * A : (z + 1) * A] = (both[C:] + off[:, z * A : (z + 1) * A]) * live
    put_halves(s_ref, sums(q_ref[...], th[...], tl[...]), keep1, send1)


def last_kernel(keep, got, kw, th, tl, hid, mask, wo, *refs):
    rad = refs[:PARTS]
    new_hid, pot_out, s_ref = refs[PARTS:]
    pot = the_potential(keep, got, kw, th, tl, s_ref)
    wot = wo[1].astype(F32).T.astype(BF)
    for z in range(CZ):
        pot_out[z] = pot[:, z * A : (z + 1) * A]
        new_hid[z] = updated(hid, pot, rad, mask, wot, z)


VM = pl.BlockSpec(memory_space=pltpu.VMEM)


def call(kernel, outs, scratch, args, flops, name, mib):
    return pl.pallas_call(
        kernel,
        out_shape=[jax.ShapeDtypeStruct(s, d) for s, d in outs],
        in_specs=[VM] * len(args),
        out_specs=[VM] * len(outs),
        scratch_shapes=scratch,
        compiler_params=pltpu.CompilerParams(vmem_limit_bytes=mib << 20),
        cost_estimate=pl.CostEstimate(flops=flops, bytes_accessed=1 << 20, transcendentals=0),
        name=name,
    )(*args)


def pairs(layer, geometry, wr, values):
    return [
        call(
            lambda *r, p=p: pair_kernel(layer, p * CHUNK, CHUNK, *r),
            [((CHUNK, C, A), F32)],
            [pltpu.VMEM((CHUNK, C, M * A), F32)],
            [*geometry, wr, *values],
            5_000_000_000,
            f"pairs{p}",
            16,
        )[0]
        for p in range(PARTS)
    ]


def flat(fn):
    pairs_ = []
    for x in range(NX):
        for y in range(NY):
            for c in range(NC):
                for z in range(NZ):
                    a, b, e, f = fn(x, y, c, z)
                    pairs_.append((((x * NY + y) * NC + c) * NZ + z, ((a * NY + b) * NC + e) * NZ + f))
    return pairs_


def moved(x, y, c, z, axis, k):
    at = {"x": x, "y": y, "z": z}
    at[axis] ^= k
    return at["x"], at["y"], c, at["z"]


PARTNER = [(i, i ^ 1) for i in range(NX * NY * NC)]
OTHER = [(i, (i + (1 if i % 2 else -1)) % (NX * NY * NC)) for i in range(NX * NY * NC)]


def all_sum(layer, keep, send, beside):
    with jax.named_scope(f"sa_L{layer}"):
        got = lax.ppermute(send, "gx", PARTNER)
    y = keep + got.astype(F32)
    for stage in range(3):
        b = y.astype(BF)
        perms = [flat(lambda x, yy, c, z: moved(x, yy, c, z, ORDERS[c][stage], k)) for k in (1, 2, 3)]
        with jax.named_scope(f"s{stage}_L{layer}"):
            recv = [lax.ppermute(b, AXES, perm) for perm in perms]
        y = b.astype(F32)
        for r in recv:
            y = y + r.astype(F32)
    with jax.named_scope(f"sb_L{layer}"):
        got = lax.ppermute(y.astype(BF), "gx", PARTNER)
    return y, got, beside


def halo(layer, own):
    up = [(i, (i + 1) % NZ) for i in range(NZ)]
    down = [(j, i) for i, j in up]
    with jax.named_scope(f"zh_L{layer}"):
        before = lax.ppermute(own, "gy", up)
        after = lax.ppermute(own, "gy", down)
    three = jnp.concatenate([own[None], before[None], after[None]], axis=0)
    with jax.named_scope(f"xh_L{layer}"):
        part = lax.ppermute(three, "gx", PARTNER)
        other = lax.ppermute(three, "gx", OTHER)
    return before, after, part, other


def on_device(feat, pos, spec, mask, table, kvec, kw, wv, wq, wr, wo):
    feat, pos, spec, mask = feat[0, 0], jnp.swapaxes(pos[0, 0], 0, 1), spec[0, 0], mask[0, 0]
    wv, wq = jnp.swapaxes(wv, 1, 2), jnp.swapaxes(wq, 1, 2)
    kw = kw[None, :]
    half = [((C // 2, 2 * K), F32), ((C // 2, 2 * K), BF)]
    args = [feat, pos, spec, mask, table, kvec, wv, wq]
    msg, off, th, tl, keep, send = call(
        first_kernel,
        [((MSG, A), BF), ((C, CZ * A), F32), ((2 * K, CZ * A), BF), ((2 * K, CZ * A), BF)] + half,
        [pltpu.VMEM((C, 2 * K), F32), pltpu.VMEM((C, CZ * A), F32)],
        args,
        3_000_000_000,
        "first",
        60,
    )
    values = (msg, *halo(0, msg))
    geometry = call(
        geometry_kernel,
        [((N_COL * A, ROWS), BF), ((3 * CZ, ROWS, A), BF)],
        [],
        list(values),
        500_000_000,
        "geometry",
        16,
    )
    keep, got, rad = all_sum(0, keep, send, pairs(0, geometry, wr, values))
    hid, vals, keep, send = call(
        middle_kernel,
        [((CZ, D, A), BF), ((CZ * C, A), BF)] + half,
        [pltpu.VMEM((C, 2 * K), F32), pltpu.VMEM((C, CZ * A), F32)],
        [keep, got, kw, th, tl, feat, mask, off, wo, wv, wq, *rad],
        3_000_000_000,
        "middle",
        16,
    )
    keep, got, rad = all_sum(1, keep, send, pairs(1, geometry, wr, (vals, *halo(1, vals))))
    hid, pot = call(
        last_kernel,
        [((CZ, D, A), BF), ((CZ, C, A), F32)],
        [pltpu.VMEM((C, 2 * K), F32)],
        [keep, got, kw, th, tl, hid, mask, wo, *rad],
        2_000_000_000,
        "last",
        16,
    )
    return hid[None, None], pot[None, None]


def solution(mesh):
    column = P("gx", "gy")
    in_specs = (column,) * 4 + (P(),) * 7
    return jax.shard_map(on_device, mesh=mesh, in_specs=in_specs, out_specs=(column, column), check_vma=False)
```

```python
import math

import jax
import jax.numpy as jnp
from jax import lax
from jax.experimental import pallas as pl
from jax.experimental.pallas import tpu as pltpu
from jax.sharding import PartitionSpec as P

F32 = jnp.float32
BF = jnp.bfloat16
CZ = 8
A = 128
D = 128
C = 64
K = 512
M = 8
NSPEC = 8
NX, NY, NC, NZ = 4, 4, 2, 4
LOG2E = math.log2(math.e)
SCALE = math.sqrt(64.0 * LOG2E)
EDGE = 64.0 * LOG2E
SIN_C = (3.14159264, -5.16771009, 2.55007766, -0.59829216, 0.07765941)
COS_C = (0.99999995, -4.93479286, 4.05841191, -1.33188016, 0.21969679)
MSG = CZ * C + 80
AXES = ("gx", "gy")
ORDERS = ("zyx", "yxz")
NT = (((1,), (1,)), ((), ()))
NN = (((1,), (0,)), ((), ()))


def dot(a, b, dims=NN):
    return lax.dot_general(a, b, dims, preferred_element_type=F32)


def split2(x):
    hi = x.astype(BF)
    return hi, (x - hi.astype(F32)).astype(BF)


def pieces(x):
    hi = x.astype(BF).astype(F32)
    rest = x - hi
    mid = rest.astype(BF).astype(F32)
    return hi, mid, rest - mid


def core():
    return lax.rem(lax.axis_index("gx"), 2)


def sums(q, th):
    qh, ql = split2(q)
    both = dot(jnp.concatenate([qh, ql], axis=0), th, NT)
    return both[:C] + both[C:]


def put_halves(s_ref, s, keep, send):
    s_ref[...] = s
    h = C // 2
    ci = core()
    keep[...] = s_ref[pl.ds(pl.multiple_of(ci * h, h), h), :]
    send[...] = s_ref[pl.ds(pl.multiple_of((1 - ci) * h, h), h), :].astype(BF)


def first_kernel(*refs):
    feat, pos, spec, mask, table, kvec, wv, wq = refs[:8]
    msg, off_ref, th, keep, send, s_ref, q_ref = refs[8:]
    wt = jnp.concatenate([wv[0], wq[0]], axis=0)
    tt = table[...].T
    for z in range(CZ):
        live = mask[z : z + 1, :].astype(F32)
        both = dot(wt, feat[z])
        msg[z * C : (z + 1) * C, :] = (both[:C] * live).astype(BF)
        sp = spec[z : z + 1, :]
        off = jnp.zeros((C, A), F32)
        for s in range(NSPEC):
            off = jnp.where(sp == s, tt[:, s : s + 1], off)
        off_ref[:, z * A : (z + 1) * A] = off
        q_ref[:, z * A : (z + 1) * A] = (both[C:] + off) * live
    parts = [pieces(pos[d]) for d in range(3)]
    rows = [parts[d][j] for j in range(3) for d in range(3)] + [jnp.zeros((8, A), F32)]
    msg[CZ * C :, :] = jnp.concatenate(rows, axis=0).astype(BF)
    k8 = jnp.concatenate([kvec[...] * (1.0 / (2.0 * math.pi)), jnp.zeros((5, K), F32)], axis=0)
    kt = k8.T
    gx = lax.axis_index("gx").astype(F32)
    gy = lax.axis_index("gy").astype(F32)
    rows = 64
    for i in range(K // rows):
        kx = jnp.broadcast_to(kt[i * rows : (i + 1) * rows, 0:1], (rows, A))
        ky = jnp.broadcast_to(kt[i * rows : (i + 1) * rows, 1:2], (rows, A))
        kz = jnp.broadcast_to(kt[i * rows : (i + 1) * rows, 2:3], (rows, A))
        for z in range(CZ):
            px = pos[0, z : z + 1, :] + gx
            py = pos[1, z : z + 1, :] + gy
            pz = pos[2, z : z + 1, :] + float(z)
            t = kx * px + ky * py + kz * pz
            u = t - jnp.round(t)
            v = u * u
            s = jnp.full((), SIN_C[4], F32)
            c = jnp.full((), COS_C[4], F32)
            for n in (3, 2, 1, 0):
                s = s * v + SIN_C[n]
                c = c * v + COS_C[n]
            s = s * u
            s2 = s + s
            sin = s2 * c
            cos = 1.0 - s2 * s
            r0 = i * rows
            cols = slice(z * A, (z + 1) * A)
            th[r0 : r0 + rows, cols] = cos.astype(BF)
            th[K + r0 : K + r0 + rows, cols] = sin.astype(BF)
    put_halves(s_ref, sums(q_ref[...], th[...]), keep, send)


WHERE = 1
PARTS = 1
CHUNK = CZ // PARTS
N_COL = 9
SHIFTS = [(0, 0), (0, -1), (0, 1)] + [(1, d) for d in (0, -1, 1)] + [(-1, d) for d in (0, -1, 1)]
ROWS = 24 * CZ
PRODUCTS = {0: 0, 2: 1, 4: 2, 6: 3}


def nine(own, before, after, part, other):
    return [own, before, after] + [part.at[i] for i in range(3)] + [other.at[i] for i in range(3)]


def sides(x, times, order, tail):
    parts = [pieces(v) for v in x]
    norm = list(pieces(x[0] * x[0] + x[1] * x[1] + x[2] * x[2]))
    one = [jnp.ones((CZ, A), F32)] * 3
    rows = [parts[d][j] if times == 1.0 else times * parts[d][j] for j in order for d in range(3)]
    return jnp.concatenate(rows + (one + norm if tail else norm + one), axis=0)


def geometry_kernel(own, before, after, part, other, ft, gs):
    sign = (1 - 2 * core()).astype(F32)

    def coords(ref):
        x = ref[CZ * C :, :].astype(F32)
        return [(x[8 * d : 8 * d + 8] + x[24 + 8 * d : 32 + 8 * d]) + x[48 + 8 * d : 56 + 8 * d] for d in range(3)]

    level = lax.rem(lax.broadcasted_iota(jnp.int32, (ROWS, A), 0), CZ)
    local = coords(own)
    for di, dz in enumerate((-1, 0, 1)):
        x = local if dz == 0 else [pltpu.roll(v, dz % CZ, 0) for v in local]
        x = [(x[0] - 0.5) * SCALE, (x[1] - 0.5) * SCALE, (x[2] - (0.5 + dz)) * SCALE]
        side = sides(x, -2.0, (0, 0, 1, 0, 2, 1), True)
        for zb in range(CZ):
            gs[di * CZ + zb] = jnp.where(level == zb, side, 0.0).astype(BF)
    for col, ref in enumerate(nine(own, before, after, part, other)):
        times, oy = SHIFTS[col]
        p = coords(ref)
        x = [(p[0] + (sign * times - 0.5)) * SCALE, (p[1] + (oy - 0.5)) * SCALE, (p[2] - 0.5) * SCALE]
        ft[col * A : (col + 1) * A, :] = sides(x, 1.0, (0, 1, 0, 2, 0, 1), False).T.astype(BF)


def pair_kernel(layer, z0, nz, ft, gs, wr, *refs):
    out, acc = refs[-2], refs[-1]
    vals = nine(*refs[:-2])
    u0 = max(3 * z0, 1)
    total = min(3 * (z0 + nz), 3 * CZ - 1) - u0
    row_ids = lax.broadcasted_iota(jnp.int32, (A, A), 0)
    col_ids = lax.broadcasted_iota(jnp.int32, (A, A), 1)

    def step(t):
        u = jnp.minimum(t, total - 1) + u0
        return lax.div(u, 3), lax.rem(u, 3) - 1

    def body_with(r0, r1, b0, b1):
        rbuf, bbuf = (r0, r1), (b0, b1)

        def distance(p, gen):
            (z, dz), (z1, dz1) = step(2 * p), step(2 * p + 1)
            both = jnp.concatenate([gs[(dz + 1) * CZ + z + dz], gs[(dz1 + 1) * CZ + z1 + dz1]], axis=1)
            r2 = dot(ft[...], both)
            for i, d in enumerate((dz, dz1)):
                part = r2[:, i * A : (i + 1) * A]
                rbuf[gen][i, :A] = jnp.where(row_ids == col_ids + d * 1024, EDGE, part[:A])
                rbuf[gen][i, A:] = part[A:]

        def basis(gen, par, col):
            for r0 in range(col * A, (col + 1) * A, 16):
                r2 = jnp.minimum(jnp.maximum(rbuf[gen][par, r0 : r0 + 16], 1e-12), EDGE)
                h = r2 * lax.rsqrt(r2) * math.sqrt(LOG2E)
                ratio = jnp.exp2(h + h)
                e = EDGE - r2
                w = jnp.exp2(h - r2) * (e * e)
                ratio2 = ratio * ratio
                odd = ratio.astype(BF)
                for m in range(0, M, 2):
                    even = w.astype(BF)
                    bbuf[par][m // 2, r0 : r0 + 16, :A] = even
                    bbuf[par][m // 2, r0 : r0 + 16, A:] = even * odd
                    if m < M - 2:
                        w = w * ratio2

        def product(t, par, j):
            z, dz = step(t)
            rows = pl.ds(pl.multiple_of((z + dz) * C, C), C)
            v = jnp.concatenate([ref[rows, :] for ref in vals], axis=1)
            acc[z - z0, :, 2 * j * A : 2 * (j + 1) * A] += dot(v, bbuf[par][j])

        def two(p, gen, old=True):
            for par in (0, 1):
                for col in range(N_COL):
                    basis(gen, par, col)
                    if par == 0 and col == WHERE:
                        distance(p + 1, 1 - gen)
                    if (old or par == 1) and col in PRODUCTS:
                        product(2 * p + par - 1, 1 - par, PRODUCTS[col])

        distance(0, 0)
        acc[...] = jnp.zeros_like(acc)
        two(0, 0, old=False)

        def body(i, carry):
            two(2 * i + 1, 1)
            two(2 * i + 2, 0)
            return carry

        lax.fori_loop(0, (total // 2 - 1) // 2, body, 0)
        for j in range(4):
            product(total - 1, 1, j)

    pl.run_scoped(
        body_with,
        pltpu.VMEM((2, N_COL * A, A), F32),
        pltpu.VMEM((2, N_COL * A, A), F32),
        pltpu.VMEM((4, N_COL * A, 2 * A), BF),
        pltpu.VMEM((4, N_COL * A, 2 * A), BF),
    )
    mix = jnp.concatenate(
        [wr[layer, m : m + 1, :] * (math.exp(-((m + 0.5) ** 2)) / EDGE**2) for m in range(M)], axis=0
    ).T
    for z in range(nz):
        r = jnp.zeros((C, A), F32)
        for m in range(M):
            r = r + acc[z, :, m * A : (m + 1) * A] * mix[:, m : m + 1]
        out[z] = r


def the_potential(keep, got, kw, th, s_ref):
    ci = core()
    h = C // 2
    s_ref[pl.ds(pl.multiple_of(ci * h, h), h), :] = keep[...]
    s_ref[pl.ds(pl.multiple_of((1 - ci) * h, h), h), :] = got[...].astype(F32)
    scale = 1.0 / math.sqrt(K * NX * NY * NC * NZ * CZ * A)
    k2 = jnp.concatenate([kw[...], kw[...]], axis=1) * scale
    wh, wl = split2(s_ref[...] * k2)
    both = dot(jnp.concatenate([wh, wl], axis=0), th[...])
    return both[:C] + both[C:]


def updated(hid, pot, rad, mask, wot, z):
    x = rad[z // CHUNK][z % CHUNK] + pot[:, z * A : (z + 1) * A]
    act = (x / (1.0 + jnp.exp(-x))).astype(BF)
    live = mask[z : z + 1, :].astype(F32)
    return (hid[z].astype(F32) + dot(wot, act) * live).astype(BF)


def middle_kernel(keep, got, kw, th, hid, mask, off, wo, wv, wq, *refs):
    rad = refs[:PARTS]
    new_hid, vals, keep1, send1, s_ref, q_ref = refs[PARTS:]
    pot = the_potential(keep, got, kw, th, s_ref)
    wot = wo[0].astype(F32).T.astype(BF)
    wt = jnp.concatenate([wv[1], wq[1]], axis=0)
    for z in range(CZ):
        h = updated(hid, pot, rad, mask, wot, z)
        new_hid[z] = h
        live = mask[z : z + 1, :].astype(F32)
        both = dot(wt, h)
        vals[z * C : (z + 1) * C, :] = (both[:C] * live).astype(BF)
        q_ref[:, z * A : (z + 1) * A] = (both[C:] + off[:, z * A : (z + 1) * A]) * live
    put_halves(s_ref, sums(q_ref[...], th[...]), keep1, send1)


def last_kernel(keep, got, kw, th, hid, mask, wo, *refs):
    rad = refs[:PARTS]
    new_hid, pot_out, s_ref = refs[PARTS:]
    pot = the_potential(keep, got, kw, th, s_ref)
    wot = wo[1].astype(F32).T.astype(BF)
    for z in range(CZ):
        pot_out[z] = pot[:, z * A : (z + 1) * A]
        new_hid[z] = updated(hid, pot, rad, mask, wot, z)


VM = pl.BlockSpec(memory_space=pltpu.VMEM)


def call(kernel, outs, scratch, args, flops, name, mib):
    return pl.pallas_call(
        kernel,
        out_shape=[jax.ShapeDtypeStruct(s, d) for s, d in outs],
        in_specs=[VM] * len(args),
        out_specs=[VM] * len(outs),
        scratch_shapes=scratch,
        compiler_params=pltpu.CompilerParams(vmem_limit_bytes=mib << 20),
        cost_estimate=pl.CostEstimate(flops=flops, bytes_accessed=1 << 20, transcendentals=0),
        name=name,
    )(*args)


def pairs(layer, geometry, wr, values):
    return [
        call(
            lambda *r, p=p: pair_kernel(layer, p * CHUNK, CHUNK, *r),
            [((CHUNK, C, A), F32)],
            [pltpu.VMEM((CHUNK, C, M * A), F32)],
            [*geometry, wr, *values],
            5_000_000_000,
            f"pairs{p}",
            16,
        )[0]
        for p in range(PARTS)
    ]


def flat(fn):
    pairs_ = []
    for x in range(NX):
        for y in range(NY):
            for c in range(NC):
                for z in range(NZ):
                    a, b, e, f = fn(x, y, c, z)
                    pairs_.append((((x * NY + y) * NC + c) * NZ + z, ((a * NY + b) * NC + e) * NZ + f))
    return pairs_


def moved(x, y, c, z, axis, k):
    at = {"x": x, "y": y, "z": z}
    at[axis] ^= k
    return at["x"], at["y"], c, at["z"]


PARTNER = [(i, i ^ 1) for i in range(NX * NY * NC)]
OTHER = [(i, (i + (1 if i % 2 else -1)) % (NX * NY * NC)) for i in range(NX * NY * NC)]


def all_sum(layer, keep, send, beside):
    with jax.named_scope(f"sa_L{layer}"):
        got = lax.ppermute(send, "gx", PARTNER)
    y = keep + got.astype(F32)
    for stage in range(3):
        b = y.astype(BF)
        perms = [flat(lambda x, yy, c, z: moved(x, yy, c, z, ORDERS[c][stage], k)) for k in (1, 2, 3)]
        with jax.named_scope(f"s{stage}_L{layer}"):
            recv = [lax.ppermute(b, AXES, perm) for perm in perms]
        y = b.astype(F32)
        for r in recv:
            y = y + r.astype(F32)
    with jax.named_scope(f"sb_L{layer}"):
        got = lax.ppermute(y.astype(BF), "gx", PARTNER)
    return y, got, beside


def halo(layer, own):
    up = [(i, (i + 1) % NZ) for i in range(NZ)]
    down = [(j, i) for i, j in up]
    with jax.named_scope(f"zh_L{layer}"):
        before = lax.ppermute(own, "gy", up)
        after = lax.ppermute(own, "gy", down)
    three = jnp.concatenate([own[None], before[None], after[None]], axis=0)
    with jax.named_scope(f"xh_L{layer}"):
        part = lax.ppermute(three, "gx", PARTNER)
        other = lax.ppermute(three, "gx", OTHER)
    return before, after, part, other


def on_device(feat, pos, spec, mask, table, kvec, kw, wv, wq, wr, wo):
    feat, pos, spec, mask = feat[0, 0], jnp.swapaxes(pos[0, 0], 0, 1), spec[0, 0], mask[0, 0]
    wv, wq = jnp.swapaxes(wv, 1, 2), jnp.swapaxes(wq, 1, 2)
    kw = kw[None, :]
    half = [((C // 2, 2 * K), F32), ((C // 2, 2 * K), BF)]
    args = [feat, pos, spec, mask, table, kvec, wv, wq]
    msg, off, th, keep, send = call(
        first_kernel,
        [((MSG, A), BF), ((C, CZ * A), F32), ((2 * K, CZ * A), BF)] + half,
        [pltpu.VMEM((C, 2 * K), F32), pltpu.VMEM((C, CZ * A), F32)],
        args,
        3_000_000_000,
        "first",
        60,
    )
    values = (msg, *halo(0, msg))
    geometry = call(
        geometry_kernel,
        [((N_COL * A, ROWS), BF), ((3 * CZ, ROWS, A), BF)],
        [],
        list(values),
        500_000_000,
        "geometry",
        16,
    )
    keep, got, rad = all_sum(0, keep, send, pairs(0, geometry, wr, values))
    hid, vals, keep, send = call(
        middle_kernel,
        [((CZ, D, A), BF), ((CZ * C, A), BF)] + half,
        [pltpu.VMEM((C, 2 * K), F32), pltpu.VMEM((C, CZ * A), F32)],
        [keep, got, kw, th, feat, mask, off, wo, wv, wq, *rad],
        3_000_000_000,
        "middle",
        16,
    )
    keep, got, rad = all_sum(1, keep, send, pairs(1, geometry, wr, (vals, *halo(1, vals))))
    hid, pot = call(
        last_kernel,
        [((CZ, D, A), BF), ((CZ, C, A), F32)],
        [pltpu.VMEM((C, 2 * K), F32)],
        [keep, got, kw, th, hid, mask, wo, *rad],
        2_000_000_000,
        "last",
        16,
    )
    return hid[None, None], pot[None, None]


def solution(mesh):
    column = P("gx", "gy")
    in_specs = (column,) * 4 + (P(),) * 7
    return jax.shard_map(on_device, mesh=mesh, in_specs=in_specs, out_specs=(column, column), check_vma=False)
```
